32 devices in a mesh: seq: 4 (over y, core), mp: 8 (over z, x).
Axes of the slice: x: 2, y: 2, z: 4, core: 2. Of those that a mesh axis runs over, the one named last changes fastest.
Arguments:
- inputs: bfloat16 [8, 1024, 2048], P('mp', 'seq'), may hold values from -6 to 6
- cotangent: bfloat16 [8, 1024, 2048], P('mp', 'seq'), may hold values from -6 to 6
- segment_ids: int32 [8, 1024], P('mp', 'seq'), may hold values from 0 to 3, never falling along the last dimension, each value on 1 to 512 neighbouring positions
- mixer_gain: bfloat16 [2048], P('mp'), may hold values from 0.5 to 1.5
- query_weight: bfloat16 [2048, 2048], P(None, 'mp'), may hold values from -0.125 to 0.125
- key_weight: bfloat16 [2048, 2048], P(None, 'mp'), may hold values from -0.125 to 0.125
- value_weight: bfloat16 [2048, 2048], P(None, 'mp'), may hold values from -0.125 to 0.125
- swish_weight: bfloat16 [2048, 2048], P(None, 'mp'), may hold values from -0.125 to 0.125
- decay_weight: bfloat16 [2048, 16], P('mp'), may hold values from -0.25 to 0.25
- decay_bias: float32 [16], replicated, may hold values from -1 to 7
- output_weight: bfloat16 [2048, 2048], P('mp'), may hold values from -0.25 to 0.25
- feed_gain: bfloat16 [2048], P('mp'), may hold values from 0.5 to 1.5
- gate_weight: bfloat16 [2048, 5504], P(None, 'mp'), may hold values from -0.125 to 0.125
- up_weight: bfloat16 [2048, 5504], P(None, 'mp'), may hold values from -0.125 to 0.125
- down_weight: bfloat16 [5504, 2048], P('mp'), may hold values from -0.15625 to 0.15625
Outputs:
- layer_out: bfloat16 [8, 1024, 2048], P('mp', 'seq')
- input_grad: bfloat16 [8, 1024, 2048], P('mp', 'seq')
- mixer_grad: float32 [2048], P('mp')
- query_grad: float32 [2048, 2048], P(None, 'mp')
- key_grad: float32 [2048, 2048], P(None, 'mp')
- value_grad: float32 [2048, 2048], P(None, 'mp')
- swish_grad: float32 [2048, 2048], P(None, 'mp')
- decay_grad: float32 [2048, 16], P('mp')
- bias_grad: float32 [16], replicated
- output_grad: float32 [2048, 2048], P('mp')
- feed_grad: float32 [2048], P('mp')
- gate_grad: float32 [2048, 5504], P(None, 'mp')
- up_grad: float32 [2048, 5504], P(None, 'mp')
- down_grad: float32 [5504, 2048], P('mp')
The draws below stay inside these ranges and needn't reach their ends.
Inputs may be any that keep to these rules, and one draw needn't show every extreme that they name: `segment_ids`: within each sequence the ids never fall; each document spans 1 to 512 tokens, and one spans exactly that many.
All inputs are finite; a program needn't handle non-finite values.
Results may differ from the reference program's by a relative error of at most 0.025.
Values may be sent and summed in bfloat16 or wider, within the bound.
No kernel may reach another device: no remote copies, remote signals or barrier semaphores. Data moves between devices by JAX's collectives and lax.ppermute only.
A program may use at most 384 MiB of HBM per device.

```python
import math
import jax
import jax.numpy as jnp
import numpy as np
from jax import lax

D = 2048
H = 16
HD = 128
FF = 5504
TOK_DEV = 256
LEN = 1024
NSEQ = 8


def shard_levels(rng, shape, cuts, smallest, top_value):
    loudness = 1.0
    for axis_at, parts in cuts:
        draws = jax.random.uniform(jax.random.fold_in(jax.random.fold_in(rng, 6), axis_at), (parts,), jnp.float32, smallest / len(cuts), top_value / len(cuts))
        loudness = loudness * jnp.repeat(jnp.exp(draws), shape[axis_at] // parts).reshape((-1,) + (1,) * (len(shape) - 1 - axis_at))
    return loudness


def split_up(amount, total, bound, slope):
    portions = [(1 << 20) // math.isqrt(rank ** slope) + 1 for rank in range(2, amount + 1)]
    rest, given = total - bound - (amount - 1), [1] * (amount - 1)
    while rest > 0:
        free = [i for i in range(amount - 1) if given[i] < bound]
        whole, left = sum([portions[i] for i in free]), rest
        for i in free:
            extra = min(bound - given[i], max(1, left * portions[i] // whole), rest)
            given[i] = given[i] + extra
            rest = rest - extra
    return np.array([bound] + given)


def ragged(rng, count, total, limit, skew):
    if count == 2:
        one = jax.random.randint(rng, (), max(1, total - limit), min(limit, total - 1) + 1)
        return jnp.stack([one, total - one])
    sizes = jnp.asarray(split_up(count, total, limit, skew), jnp.int32)
    pairs = (count - 1) // 2
    donor, sink = sizes[1:1 + 2 * pairs:2], sizes[2:2 + 2 * pairs:2]
    margin = jnp.minimum(donor - 1, limit - sink)
    passed = jax.random.randint(jax.random.fold_in(rng, 1), (pairs,), 0, 1 << 20) % (margin + 1)
    sizes = sizes.at[1:1 + 2 * pairs:2].set(donor - passed).at[2:2 + 2 * pairs:2].set(sink + passed)
    return sizes[jax.random.permutation(jax.random.fold_in(rng, 2), count)]


def bell_draw(own_key, shape, deviation, reach, split=(), held_as=jnp.bfloat16):
    array = jax.random.normal(own_key, shape, jnp.float32) * deviation
    if len(split) > 0:
        array = shard_levels(own_key, shape, split, -0.22, 0.18) * array
    return jnp.clip(array, min=-reach, max=reach).astype(held_as)


def setup_inputs(seed: int = 0) -> dict:
    key_list = jax.random.split(jax.random.key(seed), 16)
    return {
        "inputs": bell_draw(key_list[0], (NSEQ, LEN, D), 1.0, 6.0, ((0, 8), (1, 4))),
        "cotangent": bell_draw(key_list[1], (NSEQ, LEN, D), 1.0, 6.0, ((0, 8), (1, 4))),
        "segment_ids": jax.vmap(lambda own: jnp.searchsorted(jnp.cumsum(ragged(own, 4, LEN, LEN // 2, 0)), jnp.arange(LEN), side="right"))(jax.random.split(key_list[2], NSEQ)).reshape((NSEQ, LEN)).astype(jnp.int32),
        "mixer_gain": jnp.clip(1.0 + 0.1 * jax.random.normal(key_list[3], (D,), jnp.float32), 0.5, 1.5).astype(jnp.bfloat16),
        "query_weight": bell_draw(key_list[4], (D, D), D ** -0.5, 0.125, ((1, 8),)),
        "key_weight": bell_draw(key_list[5], (D, D), D ** -0.5, 0.125, ((1, 8),)),
        "value_weight": bell_draw(key_list[6], (D, D), D ** -0.5, 0.125, ((1, 8),)),
        "swish_weight": bell_draw(key_list[7], (D, D), D ** -0.5, 0.125, ((1, 8),)),
        "decay_weight": bell_draw(key_list[8], (D, H), (D // 4) ** -0.5, 0.25, ((0, 8),)),
        "decay_bias": jnp.clip(jax.random.uniform(key_list[9], (H,), jnp.float32, -1.0, 7.0), -1.0, 7.0),
        "output_weight": bell_draw(key_list[10], (D, D), (D // 4) ** -0.5, 0.25, ((0, 8),)),
        "feed_gain": jnp.clip(1.0 + 0.1 * jax.random.normal(key_list[11], (D,), jnp.float32), 0.5, 1.5).astype(jnp.bfloat16),
        "gate_weight": bell_draw(key_list[12], (D, FF), D ** -0.5, 0.125, ((1, 8),)),
        "up_weight": bell_draw(key_list[13], (D, FF), D ** -0.5, 0.125, ((1, 8),)),
        "down_weight": bell_draw(key_list[14], (FF, D), (FF // 4) ** -0.5, 0.15625, ((0, 8),)),
    }


highest = lax.Precision.HIGHEST
rms_eps = 1e-06
group_eps = 16.0

@jax.custom_vjp
def low(v):
    return lax.optimization_barrier(v.astype(jnp.bfloat16)).astype(jnp.float32)

@jax.custom_vjp
def low_back(v):
    return v

def low_keep(v):
    return (low(v), None)

def low_pass(kept, grad):
    return (grad,)

def back_keep(v):
    return (v, None)

def back_low(kept, grad):
    return (low(grad),)
low.defvjp(low_keep, low_pass)
low_back.defvjp(back_keep, back_low)

def matmul(left_side, right_side):
    return jnp.dot(left_side, right_side, precision=highest, preferred_element_type=jnp.float32)

def rms_norm(source, gain_row):
    scaling = lax.rsqrt(lax.optimization_barrier(jnp.mean(source * source, axis=-1, keepdims=True)) + rms_eps)
    return source * scaling * gain_row

def local_out(queries, key_rows, values, decays, incoming, segment, previous):
    kind = queries.dtype
    cumulative = jnp.cumsum(decays, axis=0)
    length_rows = segment.shape[0]
    positions = jnp.arange(length_rows, dtype=jnp.int32)
    causal = (positions[:, None] >= positions[None, :]) & (segment[:, None] == segment[None, :])
    differ = cumulative.T[:, :, None] - cumulative.T[:, None, :]
    weights = jnp.where(causal[None], jnp.exp(jnp.minimum(differ, jnp.zeros((), kind))), jnp.zeros((), kind))
    scores = jnp.einsum('thd,shd->hts', queries, key_rows, precision=highest) * weights
    outputs = jnp.einsum('hts,she->the', scores, values, precision=highest)
    same_doc = (segment == previous.astype(jnp.int32)).astype(kind)
    entry_decay = jnp.exp(cumulative) * same_doc[:, None]
    return outputs + entry_decay[:, :, None] * jnp.einsum('thd,hde->the', queries, incoming, precision=highest)

def local_tail(key_rows, values, decays, segment, previous):
    kind = key_rows.dtype
    cumulative = jnp.cumsum(decays, axis=0)
    last_index = segment.shape[0] - 1
    last_id = segment[last_index].astype(jnp.int32)
    final_sum = cumulative[last_index]
    carry_keep = jnp.exp(final_sum) * (last_id == previous.astype(jnp.int32)).astype(kind)
    tail_decay = jnp.exp(final_sum[None, :] - cumulative) * (segment == last_id)[:, None].astype(kind)
    tail_states = jnp.einsum('shd,she->hde', key_rows * tail_decay[:, :, None], values, precision=highest)
    return (carry_keep, tail_states)

def retention_block(carried, pieces):
    states, previous = carried
    queries, key_rows, values, decays, segment = pieces
    outputs = local_out(queries, key_rows, values, decays, states, segment, previous)
    carry_keep, tail_states = local_tail(key_rows, values, decays, segment, previous)
    last_id = segment[segment.shape[0] - 1].astype(jnp.int32)
    new_states = (carry_keep[:, None, None] * states + tail_states).astype(states.dtype)
    return ((new_states, last_id), outputs)

def sequence_retention(pieces):
    queries, key_rows, values, decays, segment = pieces
    blocks = int(LEN // TOK_DEV)

    def split_rows(tensor):
        return tensor.reshape((blocks, TOK_DEV) + tuple(tensor.shape[1:]))
    initial = (jnp.zeros((H, HD, HD), dtype=queries.dtype), jnp.zeros((), dtype=jnp.int32))
    finals, outputs = lax.scan(jax.checkpoint(retention_block), initial, (split_rows(queries), split_rows(key_rows), split_rows(values), split_rows(decays), split_rows(segment.astype(jnp.int32))))
    return outputs.reshape(LEN, H, HD)

def forward(tokens, mixer_gain, query_weight, key_weight, value_weight, swish_weight, decay_weight, decay_bias, output_weight, feed_gain, gate_weight, up_weight, down_weight, segment_ids):
    normed = low(rms_norm(tokens, mixer_gain))
    queries = low(low_back(matmul(normed, query_weight)))
    key_rows = low(low_back(matmul(normed, key_weight)))
    values = low(low_back(matmul(normed, value_weight)))
    swish_pre = low_back(matmul(normed, swish_weight))
    decay_pre = low_back(matmul(normed, decay_weight)) + decay_bias
    decays = -jax.nn.softplus(-decay_pre) / 16.0
    shaped = (NSEQ, LEN, H, HD)
    retained = lax.map(sequence_retention, (queries.reshape(shaped), key_rows.reshape(shaped), values.reshape(shaped), decays.reshape(NSEQ, LEN, H), segment_ids.astype(jnp.int32)))
    retained = retained.reshape(NSEQ * LEN, H, HD)
    centered = retained - lax.optimization_barrier(jnp.mean(retained, axis=-1, keepdims=True))
    grouped = centered * lax.rsqrt(lax.optimization_barrier(jnp.mean(centered * centered, axis=-1, keepdims=True)) + group_eps)
    gated = low(grouped.reshape(NSEQ * LEN, D) * jax.nn.silu(swish_pre))
    mixed = tokens + low_back(matmul(gated, output_weight))
    normed_two = low(rms_norm(mixed, feed_gain))
    gate_pre = low_back(matmul(normed_two, gate_weight))
    up_pre = low_back(matmul(normed_two, up_weight))
    hidden = low(jax.nn.silu(gate_pre) * up_pre)
    return mixed + low_back(matmul(hidden, down_weight))

def reference(inputs, cotangent, segment_ids, mixer_gain, query_weight, key_weight, value_weight, swish_weight, decay_weight, decay_bias, output_weight, feed_gain, gate_weight, up_weight, down_weight):
    floats = tuple((tensor.astype(jnp.float32) for tensor in (inputs.reshape(NSEQ * LEN, D), mixer_gain, query_weight, key_weight, value_weight, swish_weight, decay_weight, decay_bias, output_weight, feed_gain, gate_weight, up_weight, down_weight)))
    segment_ints = segment_ids.astype(jnp.int32)

    def closed(*params):
        return forward(*params, segment_ints)
    result, pullback = jax.vjp(closed, *floats)
    grads = pullback(cotangent.reshape(NSEQ * LEN, D).astype(jnp.float32))
    return (result.reshape(NSEQ, LEN, D).astype(jnp.bfloat16), grads[0].reshape(NSEQ, LEN, D).astype(jnp.bfloat16), grads[1], grads[2], grads[3], grads[4], grads[5], grads[6], grads[7], grads[8], grads[9], grads[10], grads[11], grads[12])
```

```python
import jax
import jax.numpy as jnp
from jax import lax
from jax.experimental import pallas as pl
from jax.experimental.pallas import tpu as pltpu
from jax.sharding import PartitionSpec as P

rms_eps = 1e-06
group_eps = 16.0
f32 = jnp.float32
bf16 = jnp.bfloat16


def dot(left, right, dims, **kw):
    return lax.dot_general(
        left, right, ((dims[0], dims[1]), ((), ())), preferred_element_type=f32, **kw
    )


def mm(left, right):
    return dot(left, right, ((1,), (0,)))


def mm_t(left, right):
    return dot(left, right, ((1,), (1,)))


def t_mm(left, right):
    return dot(left, right, ((0,), (0,)))


def silu_slope(pre_act):
    logistic = jax.nn.sigmoid(pre_act)
    return logistic * (1.0 + pre_act * (1.0 - logistic))


class Place:
    def __init__(self):
        self.seq_ways, self.ways = lax.axis_size("seq"), lax.axis_size("mp")
        seat = lax.axis_index("seq")
        self.rank = lax.axis_index("mp")
        self.row, self.core = seat >> 1, seat & 1
        self.rows = self.seq_ways // 2
        self.side = self.row & 1
        self.top = self.ways // 2
        self.lows = [1 << b for b in range(self.ways.bit_length() - 2) if (1 << b) != 2]

    def hop(self, value, where):
        pairs = []
        for seat in range(self.seq_ways):
            for rank in range(self.ways):
                to = where(seat // 2, seat % 2, rank)
                if to is not None:
                    pairs.append((seat * self.ways + rank, (to[0] * 2 + to[1]) * self.ways + to[2]))
        return lax.ppermute(value, ("seq", "mp"), pairs)

    def other_core(self, value):
        return self.hop(value, lambda y, c, m: (y, 1 - c, m))

    def partner(self, value):
        return self.hop(value, lambda y, c, m: (y, c, m ^ 2))

    def over(self, value, bit):
        return self.hop(value, lambda y, c, m: (y, c, m ^ bit))


def halves(value, axis):
    size = value.shape[axis] // 2
    return (
        lax.slice_in_dim(value, 0, size, axis=axis),
        lax.slice_in_dim(value, size, 2 * size, axis=axis),
    )


def pick(flag, first, second):
    return jnp.where(flag == 0, first, second)


def after(value, *tokens):
    tokens = [t for t in tokens if t is not None]
    return lax.optimization_barrier((value, *tokens))[0] if tokens else value


def joined(at, got, other, axis):
    return jnp.concatenate([pick(at.side, got, other), pick(at.side, other, got)], axis=axis)


def gather_weight(at, weight, axis, shared):
    low, high = halves(weight, axis)
    got = at.hop(
        pick(at.side, low, high), lambda y, c, m: (y, c, m ^ at.top) if c == 1 else None
    )
    other = at.hop(got, lambda y, c, m: (y ^ 1, c, m) if c == 1 else None)
    shards = [pick(at.core, weight, joined(at, got, other, axis))]
    for bit in at.lows:
        if shared:
            more = []
            for shard in shards:
                low, high = halves(shard, axis)
                got = at.over(pick(at.side, low, high), bit)
                more.append(joined(at, got, at.hop(got, lambda y, c, m: (y ^ 1, c, m)), axis))
            shards = shards + more
        else:
            shards = shards + [at.over(shard, bit) for shard in shards]
    return shards


def reduce_grad(at, grads, axis, tokens=(None, None, None)):
    parts = list(grads)
    for bit in reversed(at.lows):
        count = len(parts) // 2
        sent = [after(at.over(part, bit), tokens[0]) for part in parts[count:]]
        parts = [(a.astype(f32) + b.astype(f32)).astype(bf16) for a, b in zip(parts[:count], sent)]
    low, high = halves(parts[0], axis)
    got = after(at.hop(pick(at.side, high, low), lambda y, c, m: (y ^ 1, c, m)), tokens[1])
    half = pick(at.side, low, high).astype(f32) + got.astype(f32)
    step = 2
    while step < at.rows:
        got = at.hop(half.astype(bf16), lambda y, c, m: (y ^ step, c, m))
        half = half + got.astype(f32)
        step = step * 2
    half = half.astype(bf16)
    moved = after(
        at.hop(half, lambda y, c, m: (y, c, m ^ at.top) if c == 1 else None), tokens[2]
    )
    half = pick(at.core, half, moved)
    first, second = halves(half, axis)
    got = at.other_core(pick(at.core, second, first))
    quarter = (pick(at.core, first, second).astype(f32) + got.astype(f32)).astype(bf16)
    across = at.hop(quarter, lambda y, c, m: (y ^ 1, c, m))
    mine = jnp.stack([pick(at.side, quarter, across), pick(at.side, across, quarter)])
    theirs = at.other_core(mine)
    even, odd = pick(at.core, mine, theirs), pick(at.core, theirs, mine)
    return jnp.concatenate([even[0], odd[0], even[1], odd[1]], axis=axis).astype(f32)


def gather_tokens(at, block):
    beyond = at.partner(block)
    return jnp.concatenate([block, at.other_core(block), beyond, at.other_core(beyond)], axis=0)


def scatter_tokens(at, part, size):
    width = part.shape[1]
    blocks = part.reshape(2, 2, size, width)
    got = at.other_core(blocks[:, 1])
    kept = blocks[:, 0].astype(f32) + got.astype(f32)
    beyond = at.partner(kept[1].astype(bf16))
    return kept[0] + beyond.astype(f32)


def ordered(at, value, size):
    blocks = value.reshape((2, 2, size) + value.shape[1:])
    turned = blocks[:, ::-1]
    return pick(at.core, blocks, turned).reshape((2, 2 * size) + value.shape[1:])


def unordered(at, value, size):
    blocks = value.reshape((2, 2, size) + value.shape[2:])
    turned = blocks[:, ::-1]
    return pick(at.core, blocks, turned).reshape((4 * size,) + value.shape[2:])


def head_lanes(h, base=0):
    return slice(base + h * head_size, base + (h + 1) * head_size)


head_size = 128


def seats(core_ref, size):
    return [pl.ds(pl.multiple_of((a ^ core_ref[0]) * size, size), size) for a in range(2)]


def decay_block(a, b, size, h, cum_ref, cum_row_ref, seg_ref, seg_row_ref):
    rows, cols = slice(a * size, (a + 1) * size), slice(b * size, (b + 1) * size)
    differ = cum_ref[0, rows, h : h + 1] - cum_row_ref[0, h : h + 1, cols]
    same = seg_ref[0, rows, :] == seg_row_ref[0, :, cols]
    if a == b:
        same = same & (
            lax.broadcasted_iota(jnp.int32, (size, size), 0)
            >= lax.broadcasted_iota(jnp.int32, (size, size), 1)
        )
    return jnp.where(same, jnp.exp(jnp.minimum(differ, 0.0)), 0.0)


def state_kernel(core_ref, qkv_ref, tail_ref, out_ref):
    size = qkv_ref.shape[0] // 2
    count = tail_ref.shape[2]
    spots = seats(core_ref, size)
    for h in range(count):
        total = jnp.zeros((head_size, head_size), f32)
        for a in range(2):
            key = qkv_ref[spots[a], head_lanes(h, count * head_size)]
            value = qkv_ref[spots[a], head_lanes(h, 2 * count * head_size)]
            tail = tail_ref[0, a * size : (a + 1) * size, h : h + 1]
            total = total + t_mm((key.astype(f32) * tail).astype(bf16), value)
        out_ref[0, h] = total


def forward_kernel(
    core_ref, qkv_ref, swish_ref, state_ref, entry_ref, cum_ref, cum_row_ref, seg_ref, seg_row_ref,
    gated_ref, out_ref,
):
    size = qkv_ref.shape[0] // 2
    count = cum_ref.shape[2]
    spots = seats(core_ref, size)
    for h in range(count):
        state = state_ref[0, h].astype(bf16)
        for a in range(2):
            query = qkv_ref[spots[a], head_lanes(h)]
            out = mm(query, state) * entry_ref[0, a * size : (a + 1) * size, h : h + 1]
            for b in range(a + 1):
                key = qkv_ref[spots[b], head_lanes(h, count * head_size)]
                value = qkv_ref[spots[b], head_lanes(h, 2 * count * head_size)]
                decay = decay_block(a, b, size, h, cum_ref, cum_row_ref, seg_ref, seg_row_ref)
                out = out + mm((mm_t(query, key) * decay).astype(bf16), value)
            out_ref[spots[a], head_lanes(h)] = out
            centered = out - jnp.mean(out, axis=-1, keepdims=True)
            inverse = lax.rsqrt(jnp.mean(centered * centered, axis=-1, keepdims=True) + group_eps)
            swish = swish_ref[spots[a], head_lanes(h)]
            gated = centered * inverse * (swish * jax.nn.sigmoid(swish))
            gated_ref[spots[a], head_lanes(h)] = gated.astype(bf16)


def norm_back_kernel(
    core_ref, grad_ref, out_ref, swish_ref, qkv_ref, entry_ref, swish_grad_ref, head_grad_ref, state_ref
):
    size = qkv_ref.shape[0] // 2
    count = entry_ref.shape[2]
    spots = seats(core_ref, size)
    for h in range(count):
        total = jnp.zeros((head_size, head_size), f32)
        for a in range(2):
            lanes = head_lanes(h)
            out = out_ref[spots[a], lanes]
            centered = out - jnp.mean(out, axis=-1, keepdims=True)
            inverse = lax.rsqrt(jnp.mean(centered * centered, axis=-1, keepdims=True) + group_eps)
            normed = centered * inverse
            swish = swish_ref[spots[a], lanes]
            grad = grad_ref[spots[a], lanes]
            logistic = jax.nn.sigmoid(swish)
            slope = logistic * (1.0 + swish * (1.0 - logistic))
            swish_grad_ref[spots[a], lanes] = (grad * normed * slope).astype(bf16)
            grouped = grad * (swish * logistic)
            head_grad = inverse * (
                grouped
                - jnp.mean(grouped, axis=-1, keepdims=True)
                - normed * jnp.mean(grouped * normed, axis=-1, keepdims=True)
            )
            low = head_grad.astype(bf16)
            head_grad_ref[spots[a], lanes] = low
            entry = entry_ref[0, a * size : (a + 1) * size, h : h + 1]
            query = qkv_ref[spots[a], lanes].astype(f32) * entry
            total = total + t_mm(query.astype(bf16), low)
        state_ref[0, h] = total


def back_kernel(
    core_ref, qkv_ref, head_grad_ref, state_ref, later_ref, entry_ref, tail_ref, cum_ref, cum_row_ref,
    seg_ref, seg_row_ref, low_ref, cum_grad_ref,
):
    size = qkv_ref.shape[0] // 2
    count = cum_ref.shape[2]
    spots = seats(core_ref, size)
    for h in range(count):
        state, later = state_ref[0, h].astype(bf16), later_ref[0, h].astype(bf16)
        query = [qkv_ref[spots[a], head_lanes(h)] for a in range(2)]
        key = [qkv_ref[spots[a], head_lanes(h, count * head_size)] for a in range(2)]
        value = [qkv_ref[spots[a], head_lanes(h, 2 * count * head_size)] for a in range(2)]
        grad = [head_grad_ref[spots[a], head_lanes(h)] for a in range(2)]
        grad_query, grad_key, grad_value = [], [], []
        for a in range(2):
            rows = slice(a * size, (a + 1) * size)
            entry, tail = entry_ref[0, rows, h : h + 1], tail_ref[0, rows, h : h + 1]
            grad_query.append(mm_t(grad[a], state) * entry)
            grad_key.append(mm_t(value[a], later) * tail)
            grad_value.append(mm(key[a], later) * tail)
        for a in range(2):
            for b in range(a + 1):
                decay = decay_block(a, b, size, h, cum_ref, cum_row_ref, seg_ref, seg_row_ref)
                scores = (mm_t(query[a], key[b]) * decay).astype(bf16)
                grad_scores = (mm_t(grad[a], value[b]) * decay).astype(bf16)
                grad_query[a] = grad_query[a] + mm(grad_scores, key[b])
                grad_key[b] = grad_key[b] + t_mm(grad_scores, query[a])
                grad_value[b] = grad_value[b] + t_mm(scores, grad[a])
        for a in range(2):
            low_ref[spots[a], head_lanes(h)] = grad_query[a].astype(bf16)
            low_ref[spots[a], head_lanes(h, count * head_size)] = grad_key[a].astype(bf16)
            low_ref[spots[a], head_lanes(h, 2 * count * head_size)] = grad_value[a].astype(bf16)
            both = query[a].astype(f32) * grad_query[a] - key[a].astype(f32) * grad_key[a]
            cum_grad_ref[0, a * size : (a + 1) * size, h : h + 1] = jnp.sum(
                both, axis=-1, keepdims=True
            )


def per_sequence(kernel, core, arrays, outs, cost):
    def spec(shape):
        if len(shape) == 2:
            return pl.BlockSpec((shape[0] // 2, shape[1]), lambda i, c: (i, 0))
        rest = tuple(shape[1:])
        return pl.BlockSpec((1,) + rest, lambda i, c: (i,) + (0,) * len(rest))

    return pl.pallas_call(
        kernel,
        grid_spec=pltpu.PrefetchScalarGridSpec(
            num_scalar_prefetch=1,
            grid=(2,),
            in_specs=[spec(x.shape) for x in arrays],
            out_specs=[spec(o.shape) for o in outs],
        ),
        out_shape=outs,
        cost_estimate=pl.CostEstimate(
            flops=cost, transcendentals=0, bytes_accessed=sum(x.size * x.dtype.itemsize for x in arrays)
        ),
        compiler_params=pltpu.CompilerParams(vmem_limit_bytes=48 * 1024 * 1024),
    )(core, *arrays)


def struct(shape, kind=f32):
    return jax.ShapeDtypeStruct(shape, kind)


def per_device(
    inputs,
    cotangent,
    segment_ids,
    mixer_gain,
    query_weight,
    key_weight,
    value_weight,
    swish_weight,
    decay_weight,
    decay_bias,
    output_weight,
    feed_gain,
    gate_weight,
    up_weight,
    down_weight,
):
    at = Place()
    tokens = inputs[0].astype(f32)
    size, width = tokens.shape
    heads = decay_bias.shape[0]
    local_heads = query_weight.shape[1] // head_size
    own_ranks = [at.rank ^ (at.core * at.top)]
    for bit in at.lows:
        own_ranks = own_ranks + [r ^ bit for r in own_ranks]

    small = jnp.concatenate(
        [decay_weight.T, mixer_gain[None], feed_gain[None]], axis=0
    )
    bit = 1
    while bit < at.ways:
        got = at.over(small, bit)
        upper = (at.rank >> (bit.bit_length() - 1)) & 1
        small = jnp.concatenate([pick(upper, small, got), pick(upper, got, small)], axis=1)
        bit = bit * 2
    gain_one = small[heads].astype(f32)[None]
    gain_two = small[heads + 1].astype(f32)[None]
    decay_rows = jnp.concatenate(
        [lax.dynamic_slice_in_dim(small, r * local_heads, local_heads, 0) for r in own_ranks], axis=0
    )
    bias_own = jnp.concatenate(
        [lax.dynamic_slice_in_dim(decay_bias, r * local_heads, local_heads, 0) for r in own_ranks]
    )

    pair_ids = jnp.concatenate([segment_ids, at.partner(segment_ids)], axis=0)
    other_ids = at.other_core(pair_ids)
    segments = jnp.concatenate(
        [pick(at.core, pair_ids, other_ids), pick(at.core, other_ids, pair_ids)], axis=1
    )
    last_ids = segments[:, -1:]
    previous = at.hop(last_ids, lambda y, c, m: (y + 1, c, m) if y + 1 < at.rows else None)

    wide = jnp.concatenate([query_weight, key_weight, value_weight], axis=1)
    weights = {
        "qkv": gather_weight(at, wide, 0, False),
        "swish": gather_weight(at, swish_weight, 0, True),
        "output": gather_weight(at, output_weight, 1, True),
        "gate": gather_weight(at, gate_weight, 0, True),
        "up": gather_weight(at, up_weight, 0, True),
        "down": gather_weight(at, down_weight, 1, True),
    }
    shards = range(len(own_ranks))
    lanes = local_heads * head_size

    tokens_all = gather_tokens(at, inputs[0])
    grad_out_all = gather_tokens(at, cotangent[0])
    scale_one = lax.rsqrt(jnp.mean(tokens * tokens, axis=-1, keepdims=True) + rms_eps)
    wide_all = tokens_all.astype(f32)
    scale_all = lax.rsqrt(jnp.mean(wide_all * wide_all, axis=-1, keepdims=True) + rms_eps)
    normed_all = (wide_all * scale_all * gain_one).astype(bf16)

    decay_pre = mm_t(normed_all, decay_rows) + bias_own
    decays = ordered(at, -jax.nn.softplus(-decay_pre) / 16.0, size)
    span = 2 * size
    cumulative = jnp.cumsum(decays, axis=1)
    total = cumulative[:, -1:]
    entry = jnp.exp(cumulative) * (segments == previous)[:, :, None].astype(f32)
    tail = jnp.exp(total - cumulative) * (segments == last_ids)[:, :, None].astype(f32)
    keep = jnp.exp(total[:, 0]) * (last_ids == previous).astype(f32)
    cum_rows = cumulative.transpose(0, 2, 1)
    core = at.core.reshape(1).astype(jnp.int32)
    seg_col, seg_row = segments[:, :, None], segments[:, None, :]
    states = struct((2, local_heads, head_size, head_size))
    unit = 2 * 2 * local_heads * head_size * size

    def retention_state(j, qkv):
        return per_sequence(
            state_kernel, core, [qkv, tail[..., heads_at(j)]], [states], 2 * unit * head_size
        )[0]

    def heads_at(j):
        return slice(j * local_heads, (j + 1) * local_heads)

    saved = []
    attn_part = None
    for j in shards:
        mine = heads_at(j)
        qkv = mm(normed_all, weights["qkv"][j]).astype(bf16)
        tail_state = retention_state(j, qkv)
        kept = keep[:, mine, None, None]
        incoming = jnp.zeros_like(tail_state)
        for _ in range(at.rows - 1):
            passed = (kept * incoming + tail_state).astype(bf16)
            incoming = at.hop(
                passed, lambda y, c, m: (y + 1, c, m) if y + 1 < at.rows else None
            ).astype(f32)
        swish_pre = mm(normed_all, weights["swish"][j])
        gated, outputs = per_sequence(
            forward_kernel,
            core,
            [qkv, swish_pre, incoming, entry[..., mine], cumulative[..., mine], cum_rows[:, mine], seg_col, seg_row],
            [struct((4 * size, lanes), bf16), struct((4 * size, lanes))],
            6 * unit * size,
        )
        part = mm(gated, weights["output"][j])
        attn_part = part if attn_part is None else attn_part + part
        saved.append((qkv, swish_pre, tail_state, incoming, outputs, gated))

    attended = scatter_tokens(at, attn_part.astype(bf16), size)
    mixed = tokens + attended
    scale_two = lax.rsqrt(jnp.mean(mixed * mixed, axis=-1, keepdims=True) + rms_eps)
    normed_two = (mixed * scale_two * gain_two).astype(bf16)
    two_all = gather_tokens(at, normed_two)

    down_part, two_part = 0.0, 0.0
    grads = {name: [] for name in weights}
    for j in shards:
        gate_pre = mm(two_all, weights["gate"][j])
        up_pre = mm(two_all, weights["up"][j])
        logistic = jax.nn.sigmoid(gate_pre)
        hidden = (gate_pre * logistic * up_pre).astype(bf16)
        down_part = down_part + mm(hidden, weights["down"][j])
        grad_hidden = mm_t(grad_out_all, weights["down"][j])
        grad_gate = (grad_hidden * up_pre * silu_slope(gate_pre)).astype(bf16)
        grad_up = (grad_hidden * gate_pre * logistic).astype(bf16)
        two_part = two_part + mm_t(grad_gate, weights["gate"][j]) + mm_t(grad_up, weights["up"][j])
        grads["down"].append(t_mm(hidden, grad_out_all).astype(bf16))
        grads["gate"].append(t_mm(two_all, grad_gate).astype(bf16))
        grads["up"].append(t_mm(two_all, grad_up).astype(bf16))
    grad_two = scatter_tokens(at, two_part.astype(bf16), size)
    base_two = mixed * scale_two
    feed_part = jnp.sum(grad_two * base_two, axis=0)
    scaled_two = grad_two * gain_two
    grad_mixed = cotangent[0].astype(f32) + scale_two * (
        scaled_two - base_two * jnp.mean(scaled_two * base_two, axis=-1, keepdims=True)
    )
    attended_all = gather_tokens(at, grad_mixed.astype(bf16))
    layer_out = (
        mixed + scatter_tokens(at, after(down_part.astype(bf16), grad_mixed), size)
    ).astype(bf16)[None]

    normed_part = 0.0
    grad_decays, marks = [], []
    for j in shards:
        mine = heads_at(j)
        qkv, swish_pre, tail_state, incoming, outputs, gated = saved[j]
        kept = keep[:, mine, None, None]
        grad_gated = mm_t(attended_all, weights["output"][j])
        grad_swish, grad_heads, own_grad = per_sequence(
            norm_back_kernel,
            core,
            [grad_gated, outputs, swish_pre, qkv, entry[..., mine]],
            [struct((4 * size, lanes), bf16), struct((4 * size, lanes), bf16), states],
            2 * unit * head_size,
        )
        grads["output"].append(t_mm(gated, attended_all).astype(bf16))
        later = jnp.zeros_like(own_grad)
        for _ in range(at.rows - 1):
            passed = (kept * later + own_grad).astype(bf16)
            later = at.hop(
                passed, lambda y, c, m: (y - 1, c, m) if y > 0 else None
            ).astype(f32)
        normed_part = normed_part + mm_t(grad_swish, weights["swish"][j])
        grads["swish"].append(t_mm(normed_all, grad_swish).astype(bf16))
        crossing = jnp.sum(later * (kept * incoming + tail_state), axis=(-2, -1))
        lows, grad_cum = per_sequence(
            back_kernel,
            core,
            [qkv, grad_heads, incoming, later, entry[..., mine], tail[..., mine], cumulative[..., mine], cum_rows[:, mine], seg_col, seg_row],
            [struct((4 * size, 3 * lanes), bf16), struct((2, span, local_heads))],
            15 * unit * size,
        )
        grad_decays.append(
            jnp.cumsum(grad_cum[:, ::-1], axis=1)[:, ::-1] + crossing[:, None]
        )
        normed_part = normed_part + mm_t(lows, weights["qkv"][j])
        grads["qkv"].append(t_mm(normed_all, lows).astype(bf16))
        marks.append((grad_heads, lows))
    grad_decay = unordered(at, jnp.concatenate(grad_decays, axis=-1), size)
    decay_pre_grad = grad_decay * jax.nn.sigmoid(-decay_pre) / 16.0
    decay_low = decay_pre_grad.astype(bf16)
    normed_part = normed_part + mm(decay_low, decay_rows)
    decay_part = t_mm(decay_low, normed_all)
    bias_part = jnp.sum(decay_pre_grad, axis=0)

    grad_normed = scatter_tokens(at, normed_part.astype(bf16), size)
    base_one = tokens * scale_one
    mixer_part = jnp.sum(grad_normed * base_one, axis=0)
    scaled_one = grad_normed * gain_one
    input_grad = (
        grad_mixed
        + scale_one
        * (scaled_one - base_one * jnp.mean(scaled_one * base_one, axis=-1, keepdims=True))
    ).astype(bf16)[None]

    pad_rows = jnp.zeros((heads, width), f32)
    pad_bias = jnp.zeros((heads,), f32)
    for i, r in enumerate(own_ranks):
        rows = slice(i * local_heads, (i + 1) * local_heads)
        pad_rows = lax.dynamic_update_slice_in_dim(pad_rows, decay_part[rows], r * local_heads, 0)
        pad_bias = lax.dynamic_update_slice_in_dim(pad_bias, bias_part[rows], r * local_heads, 0)
    piece = width // at.ways
    bias_row = jnp.tile(jnp.pad(pad_bias, (0, piece - heads)), at.ways)
    sums = jnp.concatenate(
        [pad_rows, mixer_part[None], feed_part[None], bias_row[None]], axis=0
    )
    bit = at.top
    while bit > 0:
        low, high = halves(sums, 1)
        upper = (at.rank >> (bit.bit_length() - 1)) & 1
        sums = pick(upper, low, high) + at.over(pick(upper, high, low), bit)
        bit = bit // 2
    sums = sums + at.other_core(sums)
    step = 1
    while step < at.rows:
        sums = sums + at.hop(sums, lambda y, c, m: (y ^ step, c, m))
        step = step * 2

    first, last = marks[0], marks[-1]
    total_of = {}
    for name in ("down", "gate", "up"):
        total_of[name] = reduce_grad(
            at, grads[name], 1 if name == "down" else 0, (attended_all, first[1], last[1])
        )
    total_of["output"] = reduce_grad(at, grads["output"], 1, (last[1], None, None))
    total_of["swish"] = reduce_grad(at, grads["swish"], 0, (last[1], None, None))
    wide_total = reduce_grad(at, grads["qkv"], 0)
    return (
        layer_out,
        input_grad,
        sums[heads],
        wide_total[:, :lanes],
        wide_total[:, lanes : 2 * lanes],
        wide_total[:, 2 * lanes :],
        total_of["swish"],
        sums[:heads].T,
        sums[heads + 2][:heads],
        total_of["output"],
        sums[heads + 1],
        total_of["gate"],
        total_of["up"],
        total_of["down"],
    )


def solution(mesh):
    placed = (
        P("mp", "seq", None),
        P("mp", "seq", None),
        P("mp", "seq"),
        P("mp"),
        P(None, "mp"),
        P(None, "mp"),
        P(None, "mp"),
        P(None, "mp"),
        P("mp", None),
        P(),
        P("mp", None),
        P("mp"),
        P(None, "mp"),
        P(None, "mp"),
        P("mp", None),
    )
    return jax.shard_map(
        per_device,
        mesh=mesh,
        in_specs=placed,
        out_specs=(
            P("mp", "seq", None),
            P("mp", "seq", None),
            P("mp"),
            P(None, "mp"),
            P(None, "mp"),
            P(None, "mp"),
            P(None, "mp"),
            P("mp", None),
            P(),
            P("mp", None),
            P("mp"),
            P(None, "mp"),
            P(None, "mp"),
            P("mp", None),
        ),
        check_vma=False,
    )
```
